32 devices in a mesh: sys: 8 (over z, core), graph: 4 (over y, x).
Axes of the slice: x: 2, y: 2, z: 4, core: 2. Of those that a mesh axis runs over, the one named last changes fastest.
Arguments:
- node_features: bfloat16 [8, 64, 25, 128], P('sys', 'graph'), may hold values from -6 to 6
- atom_slot: int32 [8, 64], P('sys'), may hold values from 0 to 63, each once within a row
- neighbour: int32 [8, 4608], P('sys', 'graph'), may hold values from 0 to 63
- pad_mask: int32 [8, 4608], P('sys', 'graph'), may hold values 0 or 1
- envelope: float32 [8, 4608], P('sys', 'graph'), may hold values from 0.1 to 1
- wigner_rows: bfloat16 [8, 13, 25, 4608], P('sys', None, None, 'graph'), may hold values from -1.1953125 to 1.1953125
- mix_table: float32 [8, 8], replicated, may hold values from 0.1 to 2
- zero_weight: bfloat16 [8, 640, 640], P('sys', 'graph'), may hold values from -0.078125 to 0.078125
- one_weight: bfloat16 [8, 512, 2, 512], P('sys', 'graph'), may hold values from -0.0625 to 0.0625
Outputs:
- update: bfloat16 [8, 64, 25, 128], P('sys', 'graph')
The draws below stay inside these ranges and needn't reach their ends.
Inputs may be any that keep to these rules, and one draw needn't show every extreme that they name: `neighbour`: atom ids of the edge's own system; edge slots a * 72 to a * 72 + 71 belong to the atom in row a of node_features. `atom_slot`: each system's row names every row of node_features once.
All inputs are finite; a program needn't handle non-finite values. No bound on the sum of `pad_mask` on one device may be relied on, other than what follows from the above.
Results may differ from the reference program's by a relative error of at most 0.025.
Values may be sent and summed in bfloat16 or wider, within the bound.
A program may use at most 64 MiB of HBM per device.

```python
import math
import jax
import jax.numpy as jnp
from jax import lax

C = 128
LMAX = 4
NEIGH = 72
SH = 25
FRAME = 13
M0 = 640
M1 = 512
EXPERTS = 8
SYSTEMS = 8
ATOMS = 64
EDGES = 4608


def touch_ends(entries, own_key, low, top_value):
    spot = [jax.random.randint(jax.random.fold_in(own_key, axis), (), 0, length) for axis, length in enumerate(entries.shape)]
    widest = entries.shape.index(max(entries.shape))
    beside = spot[:widest] + [(spot[widest] + 1) % entries.shape[widest]] + spot[widest + 1:]
    return entries.at[tuple(spot)].set(low).at[tuple(beside)].set(top_value)


def shard_levels(stream_key, dims, shards, smallest, high):
    def one(axis_at, parts):
        heights = jax.random.uniform(jax.random.fold_in(jax.random.fold_in(stream_key, 6), axis_at), (parts,), jnp.float32, smallest / len(shards), high / len(shards))
        return jnp.repeat(jnp.exp(heights), dims[axis_at] // parts).reshape((-1,) + (1,) * (len(dims) - axis_at - 1))

    loudness = one(*shards[0])
    for cut in shards[1:]:
        loudness = loudness * one(*cut)
    return loudness


def gaussian(key, shape, deviation, bound, split=(), held_as=jnp.bfloat16):
    loudness = shard_levels(key, shape, split, -0.22, 0.18) if split else 1.0
    array = jax.random.normal(key, shape, jnp.float32) * deviation * loudness
    return jnp.minimum(jnp.maximum(array, -bound), bound).astype(held_as)


def setup_inputs(seed: int = 0) -> dict:
    arg_keys = jax.random.split(jax.random.key(seed), 10)
    return {
        "node_features": gaussian(arg_keys[0], (SYSTEMS, ATOMS, SH, C), 1.0, 6.0, ((0, 8), (1, 4))),
        "atom_slot": jax.vmap(lambda own: jax.random.permutation(own, ATOMS))(jax.random.split(arg_keys[1], SYSTEMS)).reshape((SYSTEMS, ATOMS)).astype(jnp.int32),
        "neighbour": touch_ends(jax.random.randint(arg_keys[2], (SYSTEMS, EDGES), 0, ATOMS), jax.random.fold_in(arg_keys[2], 1), 0, ATOMS - 1).astype(jnp.int32),
        "pad_mask": touch_ends((jax.random.randint(arg_keys[3], (SYSTEMS, EDGES), 0, 8) < 7).astype(jnp.int32), jax.random.fold_in(arg_keys[3], 1), 0, 1),
        "envelope": jnp.clip(jnp.exp(math.log(1.0) - 2.3025851 * jax.random.uniform(arg_keys[4], (SYSTEMS, EDGES), jnp.float32) ** shard_levels(arg_keys[4], (SYSTEMS, EDGES), ((0, 8), (1, 4)), -0.2, 0.2)), 0.1, 1.0),
        "wigner_rows": gaussian(arg_keys[5], (SYSTEMS, FRAME, SH, EDGES), 0.2, 1.1953125, ((0, 8), (3, 4))),
        "mix_table": jnp.clip(jnp.exp(jax.random.uniform(arg_keys[6], (SYSTEMS, EXPERTS), jnp.float32, math.log(0.1), math.log(2.0))), 0.1, 2.0),
        "zero_weight": gaussian(arg_keys[7], (EXPERTS, M0, M0), (M0 * EXPERTS) ** -0.5, 0.078125, ((0, 8), (1, 4))),
        "one_weight": gaussian(arg_keys[8], (EXPERTS, M1, 2, M1), (2 * M1 * EXPERTS) ** -0.5, 0.0625, ((0, 8), (1, 4))),
    }


def scaled_term(factor, weight):
    term = (factor * weight.astype(jnp.float32)).astype(jnp.bfloat16)
    term = lax.optimization_barrier(term)
    return term.astype(jnp.float32)

def one_system(inputs):
    features, slots, neighbour, pad_mask, envelope, wigner, merged_zero, merged_one = inputs
    source = jnp.take(slots, neighbour, axis=0)
    gathered = jnp.take(features, source, axis=0)
    rotated = jnp.einsum('rke,ekc->erc', wigner.astype(jnp.float32), gathered.astype(jnp.float32)).astype(jnp.bfloat16)
    edge_count = rotated.shape[0]
    channels = rotated.shape[2]
    first = rotated[:, :LMAX + 1].reshape(edge_count, -1)
    plus_part = rotated[:, LMAX + 1:2 * LMAX + 1].reshape(edge_count, -1)
    minus_part = rotated[:, 2 * LMAX + 1:].reshape(edge_count, -1)
    edge_gate = envelope * pad_mask.astype(jnp.float32)
    real_part = merged_one[:, 0, :]
    imag_part = merged_one[:, 1, :]
    out_zero = jnp.dot(first, merged_zero.T, preferred_element_type=jnp.float32)
    out_plus = jnp.dot(plus_part, real_part.T, preferred_element_type=jnp.float32) - jnp.dot(minus_part, imag_part.T, preferred_element_type=jnp.float32)
    out_minus = jnp.dot(plus_part, imag_part.T, preferred_element_type=jnp.float32) + jnp.dot(minus_part, real_part.T, preferred_element_type=jnp.float32)
    out_zero = (edge_gate[:, None] * out_zero).astype(jnp.bfloat16)
    out_plus = (edge_gate[:, None] * out_plus).astype(jnp.bfloat16)
    out_minus = (edge_gate[:, None] * out_minus).astype(jnp.bfloat16)
    message = jnp.concatenate([out_zero.reshape(edge_count, LMAX + 1, channels), out_plus.reshape(edge_count, LMAX, channels), out_minus.reshape(edge_count, LMAX, channels)], axis=1)
    atom_count = edge_count // NEIGH
    total = jnp.einsum('rkaj,ajrc->akc', wigner.astype(jnp.float32).reshape(wigner.shape[0], wigner.shape[1], atom_count, NEIGH), message.astype(jnp.float32).reshape(atom_count, NEIGH, message.shape[1], channels))
    return (total * (1.0 / math.sqrt(NEIGH))).astype(jnp.bfloat16)

def reference(node_features, atom_slot, neighbour, pad_mask, envelope, wigner_rows, mix_table, zero_weight, one_weight):
    systems = mix_table.shape[0]

    def add_expert(totals, inputs):
        weight_zero, weight_one, column = inputs
        total_zero, total_one = totals
        total_zero = total_zero + scaled_term(column[:, None, None], weight_zero[None])
        total_one = total_one + scaled_term(column[:, None, None, None], weight_one[None])
        return ((total_zero, total_one), None)
    start = (jnp.zeros((systems,) + zero_weight.shape[1:], jnp.float32), jnp.zeros((systems,) + one_weight.shape[1:], jnp.float32))
    (merged_zero, merged_one), _ = lax.scan(add_expert, start, (zero_weight, one_weight, mix_table.T))
    merged_zero = merged_zero.astype(jnp.bfloat16)
    merged_one = merged_one.astype(jnp.bfloat16)
    return lax.map(one_system, (node_features, atom_slot, neighbour, pad_mask, envelope, wigner_rows, merged_zero, merged_one))
```

```python
import functools
import math

import jax
import jax.numpy as jnp
from jax import lax
from jax.experimental import pallas as pl
from jax.experimental.pallas import tpu as pltpu
from jax.sharding import PartitionSpec as P

NEIGH = 72
CORES = 2
LANES = 128
WIDE = 256
UNIT = 16
WINDOW = 5
LAG = 2
STEPS = 2
FRAMES_OF_ZERO = 5
MESH = pl.DeviceIdType.MESH


def kernel(
    chips,
    peers,
    pieces,
    feat_ref,
    slot_ref,
    near_ref,
    mask_ref,
    envelope_ref,
    frame_ref,
    mix_ref,
    zero_ref,
    one_ref,
    out_ref,
    feats,
    pair,
    own_one,
    raw_zero,
    raw_one,
    here_zero,
    here_one,
    res_zero,
    res_one,
    map_zero,
    map_one,
    local_sem,
    feat_send,
    feat_recv,
    raw_send,
    raw_recv,
    here_send,
    near_recv,
    map_send,
    map_recv,
    frame_ref_in,
    chosen,
    gate_ref,
    rows32,
    lined,
    turned,
    padded,
    rows_of,
    picked,
    rotated,
    message,
    stacked,
    summed,
):
    experts = chips * CORES
    sys_index = lax.axis_index("sys")
    graph_index = lax.axis_index("graph")
    chip = sys_index // CORES
    core = sys_index % CORES
    last = chips - 1
    partner = chip * CORES + 1 - core
    is_inner = jnp.logical_and(chip > 0, chip < last)
    is_end = jnp.logical_or(chip == 0, chip == last)
    by_end = jnp.logical_or(chip == 1, chip == last - 1)
    end_chip = jnp.where(chip <= 1, 0, last)
    spots = peers * CORES
    my_spot = graph_index * CORES + core

    barrier = pltpu.get_barrier_semaphore()

    def greet(target_sys, target_graph):
        pl.semaphore_signal(
            barrier, inc=1, device_id=(target_sys, target_graph), device_id_type=MESH
        )

    def column(act, inner_only):
        for t in range(1 if inner_only else 0, last if inner_only else chips):
            @pl.when(chip != t)
            def _():
                for h in range(CORES):
                    act(t * CORES + h, h)

    def greet_z(target, h):
        greet(target, graph_index)

    @pl.when(is_inner)
    def _():
        column(greet_z, False)

    @pl.when(is_end)
    def _():
        column(greet_z, True)

    greet(partner, graph_index)
    for step in range(1, peers):
        for h in range(CORES):
            greet(chip * CORES + h, lax.rem(graph_index + step, peers))
    greeted = 1 + CORES * (peers - 1) + CORES * jnp.where(is_inner, chips - 1, chips - 2)

    own_zero = pltpu.make_async_copy(
        zero_ref.at[core], raw_zero.at[sys_index], local_sem.at[0]
    )
    own_feat = pltpu.make_async_copy(feat_ref, feats.at[graph_index], local_sem.at[1])
    own_frame = pltpu.make_async_copy(frame_ref, frame_ref_in, local_sem.at[2])
    own_zero.start()
    own_feat.start()
    own_frame.start()
    pl.semaphore_wait(barrier, greeted)

    def units(j):
        return pl.ds(pieces[j][1], pieces[j][2])

    def is_zero(j):
        return pieces[j][0] == "zero"

    def pick(j, zero, one):
        return zero if is_zero(j) else one

    def remote(source, target, send, recv, system, graph):
        return pltpu.make_async_remote_copy(
            src_ref=source,
            dst_ref=target,
            send_sem=send,
            recv_sem=recv,
            device_id=(system, graph),
            device_id_type=MESH,
        )

    def wait_bytes(ref, sem):
        pltpu.make_async_copy(ref, ref, sem).wait()

    def raw_copy(j, target, half):
        return remote(
            pick(j, zero_ref, own_one).at[half, units(j)],
            pick(j, raw_zero, raw_one).at[sys_index, units(j)],
            raw_send.at[j],
            raw_recv.at[j],
            target,
            graph_index,
        )

    def send_raw(j):
        column(lambda target, h: raw_copy(j, target, h).start(), True)

        @pl.when(is_inner)
        def _():
            raw_copy(j, partner, 1 - core).start()

    def wait_raw_sent(j):
        raw = pick(j, raw_zero, raw_one)
        inner = CORES * (chips - 3) + 1
        end = CORES * (chips - 2)

        @pl.when(is_inner)
        def _():
            wait_bytes(raw.at[0:inner, units(j)], raw_send.at[j])

        @pl.when(is_end)
        def _():
            wait_bytes(raw.at[0:end, units(j)], raw_send.at[j])

    def feat_copy(step):
        return remote(
            feat_ref,
            feats.at[graph_index],
            feat_send,
            feat_recv,
            sys_index,
            lax.rem(graph_index + step, peers),
        )

    zero_pieces = [j for j in range(len(pieces)) if is_zero(j)]
    one_pieces = [j for j in range(len(pieces)) if not is_zero(j)]
    for j in zero_pieces[:WINDOW]:
        send_raw(j)
    for step in range(1, peers):
        feat_copy(step).start()

    one_units, one_rows = own_one.shape[1], own_one.shape[2]
    pair[...] = one_ref[...].astype(jnp.float32)
    for half in range(CORES):
        for u in range(one_units):
            at = (half * (one_units // 2) + u // 2) * one_rows
            own_one[half, u] = pair[at : at + one_rows, u % 2, :].astype(jnp.bfloat16)
    for j in one_pieces:
        if j < WINDOW:
            send_raw(j)
    raw_one[sys_index] = own_one[core]
    own_zero.wait()

    def here_copy(j):
        return remote(
            pick(j, here_zero, here_one).at[:, units(j)],
            pick(j, res_zero, res_one).at[:, units(j)],
            here_send.at[j],
            near_recv.at[j],
            end_chip * CORES + core,
            graph_index,
        )

    def map_copy(j, h, step):
        return remote(
            pick(j, res_zero, res_one).at[h, units(j)],
            pick(j, map_zero, map_one).at[units(j), my_spot],
            map_send.at[j],
            map_recv.at[j],
            chip * CORES + h,
            lax.rem(graph_index + step, peers),
        )

    def mix_units(j, inputs, outputs):
        raw = pick(j, raw_zero, raw_one)
        _, begin, count = pieces[j][:3]
        strips = raw.shape[3] // LANES

        def body(i, carry):
            u = begin + i // strips
            lanes = pl.ds(pl.multiple_of((i % strips) * LANES, LANES), LANES)
            sums = [None] * len(outputs)
            for e in inputs:
                term = raw[e, u, :, lanes].astype(jnp.float32)
                for n, (system, _, _) in enumerate(outputs):
                    part = mix_ref[system, e] * term
                    sums[n] = part if sums[n] is None else sums[n] + part
            for n, (_, ref, at) in enumerate(outputs):
                ref[at, u, :, lanes] = sums[n].astype(jnp.bfloat16)
            return carry

        lax.fori_loop(0, count * strips, body, 0)

    def mix_all(j):
        res, here = pick(j, res_zero, res_one), pick(j, here_zero, here_one)
        mix_units(
            j,
            range(experts),
            [(chip * CORES + h, res, h) for h in range(CORES)]
            + [(end_chip * CORES + h, here, h) for h in range(CORES)],
        )

        @pl.when(by_end)
        def _():
            here_copy(j).start()

    def first_half(j):
        raw = pick(j, raw_zero, raw_one)

        @pl.when(is_inner)
        def _():
            wait_bytes(raw.at[0 : experts - 1, units(j)], raw_recv.at[j])
            mix_all(j)

    def second_half(j):
        res = pick(j, res_zero, res_one)

        @pl.when(is_end)
        def _():
            here_copy(j).wait_recv()

        for step in range(1, peers):
            for h in range(CORES):
                map_copy(j, h, step).start()
        for h in range(CORES):

            @pl.when(core != h)
            def _():
                map_copy(j, h, 0).start()

            @pl.when(core == h)
            def _():
                pick(j, map_zero, map_one)[units(j), my_spot] = res[h, units(j)]

    def wait_map(j):
        maps = pick(j, map_zero, map_one)
        wait_bytes(maps.at[units(j), 0 : spots - 1], map_recv.at[j])

    def wait_sent(j):
        if j + WINDOW >= total:
            wait_raw_sent(j)

        @pl.when(by_end)
        def _():
            here_copy(j).wait_send()

        maps = pick(j, map_zero, map_one)
        wait_bytes(maps.at[units(j), 0 : spots - 1], map_send.at[j])

    total = len(pieces)

    def advance(i):
        if i < total:
            first_half(i)
            if i + WINDOW < total:
                wait_raw_sent(i)
                send_raw(i + WINDOW)
        if LAG <= i < total + LAG:
            second_half(i - LAG)

    atoms = slot_ref.shape[1]
    edges = near_ref.shape[1]
    harmonics, frames = frame_ref.shape[0], frame_ref.shape[1]
    channels = feat_ref.shape[2]
    tiles = edges // LANES
    groups = LANES // UNIT
    spread = LANES // UNIT
    layers = -(-harmonics // spread)
    order_zero = FRAMES_OF_ZERO * channels
    side = one_ref.shape[2]
    wide = spread * LANES

    gate_ref[...] = envelope_ref[...] * mask_ref[...].astype(jnp.float32)
    by_id = (
        lax.broadcasted_iota(jnp.int32, (atoms, edges), 0) == near_ref[...]
    ).astype(jnp.bfloat16)
    by_slot = (
        lax.broadcasted_iota(jnp.int32, (atoms, atoms), 0) == slot_ref[...]
    ).astype(jnp.bfloat16)
    chosen[...] = jnp.dot(by_slot, by_id, preferred_element_type=jnp.float32).astype(
        jnp.bfloat16
    )
    own_frame.wait()

    def lay_tile(t, carry):
        lanes = pl.ds(pl.multiple_of(t * LANES, LANES), LANES)
        for m in range(layers):
            rows = pl.ds(pl.multiple_of((t * layers + m) * UNIT, UNIT), UNIT)
            for i in range(spread):
                k = m * spread + i
                at = slice(i * LANES, (i + 1) * LANES)
                if k < harmonics:
                    rows32[k, :frames] = frame_ref_in[k, :, lanes].astype(jnp.float32)
                    lined[rows, at] = rows32[k].astype(jnp.bfloat16)
                else:
                    lined[rows, at] = jnp.zeros((UNIT, LANES), jnp.bfloat16)
        for r in range(frames):
            padded[r, :harmonics, lanes] = rows32[:, r, :].astype(jnp.bfloat16)
        return carry

    rows32[...] = jnp.zeros_like(rows32)
    lax.fori_loop(0, tiles, lay_tile, 0)

    def turn(n, carry):
        begin = pl.multiple_of(n * WIDE, WIDE)
        source = lax.broadcasted_iota(jnp.int32, (wide, WIDE), 0)
        target = lax.broadcasted_iota(jnp.int32, (wide, WIDE), 1) + begin
        moved = (
            source % LANES // UNIT * LANES + source // LANES * UNIT + source % UNIT
        )
        swap = (moved == target).astype(jnp.bfloat16)
        turned[:, :, pl.ds(begin, WIDE)] = jnp.dot(
            lined[...], swap, preferred_element_type=jnp.float32
        ).reshape(tiles * layers, UNIT, WIDE)
        return carry

    lax.fori_loop(0, wide // WIDE, turn, 0)
    for q in range(groups):
        picked[q, harmonics * UNIT :] = jnp.zeros(
            (picked.shape[1] - harmonics * UNIT, channels), jnp.bfloat16
        )

    own_feat.wait()
    wait_bytes(feats.at[0 : peers - 1], feat_recv)
    for k in range(harmonics):
        rows_of[:, k * channels : (k + 1) * channels] = feats[:, k].reshape(atoms, channels)

    diagonal = (
        lax.broadcasted_iota(jnp.int32, (UNIT, LANES), 1) % UNIT
        == lax.broadcasted_iota(jnp.int32, (UNIT, LANES), 0)
    ).astype(jnp.float32)

    def rotate_tile(t, carry):
        lanes = pl.ds(pl.multiple_of(t * LANES, LANES), LANES)
        hot = chosen[:, lanes]
        for k in range(0, harmonics, 2):
            width = min(2, harmonics - k) * channels
            block = lax.dot_general(
                hot,
                rows_of[:, k * channels : k * channels + width],
                (((0,), (0,)), ((), ())),
                preferred_element_type=jnp.float32,
            ).astype(jnp.bfloat16)
            for q in range(groups):
                for d in range(width // channels):
                    picked[q, (k + d) * UNIT : (k + d + 1) * UNIT, :] = block[
                        q * UNIT : (q + 1) * UNIT, d * channels : (d + 1) * channels
                    ]
        for q in range(groups):
            left = []
            for r in range(frames):
                pieces_of = []
                for m in range(layers):
                    row = turned[t * layers + m, r : r + 1, q * LANES : (q + 1) * LANES]
                    pieces_of.append((row * diagonal).astype(jnp.bfloat16))
                left.append(jnp.concatenate(pieces_of, axis=1))
            result = jnp.dot(
                jnp.concatenate(left, axis=0), picked[q], preferred_element_type=jnp.float32
            ).astype(jnp.bfloat16)
            rows = pl.ds(pl.multiple_of(t * LANES + q * UNIT, UNIT), UNIT)
            for r in range(frames):
                rotated[rows, r * channels : (r + 1) * channels] = result[
                    r * UNIT : (r + 1) * UNIT
                ]
        for i in range(total + LAG):
            tile = min(i // STEPS, tiles)

            @pl.when(t == tile)
            def _():
                advance(i)

        return carry

    lax.fori_loop(0, tiles, rotate_tile, 0)
    for i in range(total + LAG):
        if i // STEPS >= tiles:
            advance(i)

    zero_rows = map_zero.shape[2]
    part_rows = map_one.shape[2]
    zero_count, one_count = map_zero.shape[0], map_one.shape[0]
    cuts = [(at, min(WIDE, edges - at)) for at in range(0, edges, WIDE)]

    def over_edges(body):
        whole = edges // WIDE

        def step(n, carry):
            body(pl.multiple_of(n * WIDE, WIDE), WIDE)
            return carry

        lax.fori_loop(0, whole, step, 0)
        if edges % WIDE:
            body(whole * WIDE, edges % WIDE)

    nt = (((1,), (1,)), ((), ()))

    def apply_zero():
        def body(at, width):
            y = lax.dot_general(
                map_zero[...].reshape(zero_count * spots * zero_rows, order_zero),
                rotated[pl.ds(at, width), :order_zero],
                nt,
                preferred_element_type=jnp.float32,
            )
            y = (gate_ref[:, pl.ds(at, width)] * y).astype(jnp.bfloat16)
            for u in range(zero_count):
                for p in range(spots):
                    base = (u * spots + p) * zero_rows
                    to = (p * zero_count + u) * zero_rows
                    message[to : to + zero_rows, pl.ds(at, width)] = y[base : base + zero_rows]

        over_edges(body)

    def apply_one(u):
        rows = spots * part_rows
        real = map_one[u].reshape(rows, side)
        imag = map_one[u + 1].reshape(rows, side)
        stacked[:rows, :side] = real
        stacked[:rows, side:] = -imag
        stacked[rows:, :side] = imag
        stacked[rows:, side:] = real

        def body(at, width):
            y = lax.dot_general(
                stacked[...],
                rotated[pl.ds(at, width), order_zero:],
                nt,
                preferred_element_type=jnp.float32,
            )
            y = (gate_ref[:, pl.ds(at, width)] * y).astype(jnp.bfloat16)
            for part in range(2):
                for p in range(spots):
                    base = part * rows + p * part_rows
                    to = order_zero + part * side + (p * (one_count // 2) + u // 2) * part_rows
                    message[to : to + part_rows, pl.ds(at, width)] = y[base : base + part_rows]

        over_edges(body)

    deep = padded.shape[1]

    def gather_back(begin, end):
        for at, width in cuts:
            first = at // NEIGH
            final = (at + width - 1) // NEIGH
            owner = lax.broadcasted_iota(jnp.int32, (deep, width), 1) + at
            masks = [
                jnp.logical_and(owner >= a * NEIGH, owner < (a + 1) * NEIGH)
                for a in range(first, final + 1)
            ]
            columns = []
            for r in range(begin, end):
                rows = padded[r, :, at : at + width]
                columns.append(
                    jnp.concatenate(
                        [jnp.where(mask, rows, jnp.zeros_like(rows)) for mask in masks], axis=0
                    )
                )
            left = jnp.concatenate(columns, axis=1)
            right = jnp.concatenate(
                [
                    message[r * channels : (r + 1) * channels, at : at + width]
                    for r in range(begin, end)
                ],
                axis=1,
            )
            product = lax.dot_general(left, right, nt, preferred_element_type=jnp.float32)
            summed[first : final + 1] += product.reshape(final + 1 - first, deep, channels)

    summed[...] = jnp.zeros_like(summed)
    for j in zero_pieces:
        wait_map(j)
    apply_zero()
    gather_back(0, FRAMES_OF_ZERO)
    for u in range(0, one_count, 2):
        for j in one_pieces:
            if u <= pieces[j][1] < u + 2:
                wait_map(j)
        apply_one(u)
    gather_back(FRAMES_OF_ZERO, frames)
    scale = 1.0 / math.sqrt(NEIGH)
    for k in range(harmonics):
        out_ref[k] = (summed[:, k, :] * scale).astype(jnp.bfloat16)

    wait_bytes(feats.at[0 : peers - 1], feat_send)
    for j in range(total):
        wait_sent(j)


def shards(systems, peers, node_features, atom_slot, neighbour, pad_mask, envelope, wigner_rows, mix_table, zero_weight, one_weight):
    chips = systems // CORES
    frames, harmonics, edges = wigner_rows.shape[1:]
    own_atoms, _, channels = node_features.shape[1:]
    zero_rows, zero_width = zero_weight.shape[1:]
    one_rows, _, side = one_weight.shape[1:]
    zero_units = max(1, zero_rows // (CORES * UNIT)) if zero_rows % (CORES * UNIT) == 0 else 1
    one_units = 2 * (max(1, one_rows // (CORES * UNIT)) if one_rows % (CORES * UNIT) == 0 else 1)
    zr = zero_rows // (CORES * zero_units)
    orr = 2 * one_rows // (CORES * one_units)
    pieces = tuple(("zero", u, 1) for u in range(zero_units)) + tuple(
        ("one", u, 1) for u in range(one_units)
    )
    atoms = own_atoms * peers
    layers = -(-harmonics // (LANES // UNIT))
    tiles = edges // LANES
    deep = -(-harmonics // 16) * 16
    spots = peers * CORES
    bf16, f32 = jnp.bfloat16, jnp.float32
    vmem = pl.BlockSpec(memory_space=pltpu.VMEM)
    hbm = pl.BlockSpec(memory_space=pl.ANY)
    smem = pl.BlockSpec(memory_space=pltpu.SMEM)
    count = len(pieces)
    update = pl.pallas_call(
        functools.partial(kernel, chips, peers, pieces),
        out_shape=jax.ShapeDtypeStruct((harmonics, own_atoms, channels), bf16),
        in_specs=[hbm, vmem, vmem, vmem, vmem, hbm, smem, hbm, vmem],
        out_specs=vmem,
        scratch_shapes=[
            pltpu.VMEM((peers, harmonics, own_atoms, channels), bf16),
            pltpu.VMEM((one_rows, 2, side), f32),
            pltpu.VMEM((CORES, one_units, orr, side), bf16),
            pltpu.VMEM((systems, zero_units, zr, zero_width), bf16),
            pltpu.VMEM((systems, one_units, orr, side), bf16),
            pltpu.VMEM((CORES, zero_units, zr, zero_width), bf16),
            pltpu.VMEM((CORES, one_units, orr, side), bf16),
            pltpu.VMEM((CORES, zero_units, zr, zero_width), bf16),
            pltpu.VMEM((CORES, one_units, orr, side), bf16),
            pltpu.VMEM((zero_units, spots, zr, zero_width), bf16),
            pltpu.VMEM((one_units, spots, orr, side), bf16),
            pltpu.SemaphoreType.DMA((3,)),
            pltpu.SemaphoreType.DMA,
            pltpu.SemaphoreType.DMA,
            pltpu.SemaphoreType.DMA((count,)),
            pltpu.SemaphoreType.DMA((count,)),
            pltpu.SemaphoreType.DMA((count,)),
            pltpu.SemaphoreType.DMA((count,)),
            pltpu.SemaphoreType.DMA((count,)),
            pltpu.SemaphoreType.DMA((count,)),
            pltpu.VMEM((harmonics, frames, edges), bf16),
            pltpu.VMEM((atoms, edges), bf16),
            pltpu.VMEM((1, edges), f32),
            pltpu.VMEM((harmonics, UNIT, LANES), f32),
            pltpu.VMEM((tiles * layers * UNIT, LANES // UNIT * LANES), bf16),
            pltpu.VMEM((tiles * layers, UNIT, LANES // UNIT * LANES), f32),
            pltpu.VMEM((frames, deep, edges), bf16),
            pltpu.VMEM((atoms, harmonics * channels), bf16),
            pltpu.VMEM((LANES // UNIT, layers * LANES, channels), bf16),
            pltpu.VMEM((edges, frames * channels), bf16),
            pltpu.VMEM((frames * channels, edges), bf16),
            pltpu.VMEM((2 * spots * orr, 2 * side), bf16),
            pltpu.VMEM((own_atoms, deep, channels), f32),
        ],
        compiler_params=pltpu.CompilerParams(
            collective_id=0, has_side_effects=True, vmem_limit_bytes=60 * 1024 * 1024
        ),
        name="edge_convolution",
    )(
        jnp.transpose(node_features[0], (1, 0, 2)),
        atom_slot,
        neighbour,
        pad_mask,
        envelope,
        jnp.transpose(wigner_rows[0], (1, 0, 2)),
        mix_table,
        zero_weight[0].reshape(CORES, zero_units, zr, zero_width),
        one_weight[0],
    )
    return jnp.transpose(update, (1, 0, 2))[None]


def solution(mesh):
    return jax.shard_map(
        functools.partial(shards, mesh.shape["sys"], mesh.shape["graph"]),
        mesh=mesh,
        in_specs=(
            P("sys", "graph", None, None),
            P("sys", None),
            P("sys", "graph"),
            P("sys", "graph"),
            P("sys", "graph"),
            P("sys", None, None, "graph"),
            P(),
            P("sys", "graph", None),
            P("sys", "graph", None, None),
        ),
        out_specs=P("sys", "graph", None, None),
        check_vma=False,
    )
```

```python
import functools
import math

import jax
import jax.numpy as jnp
from jax import lax
from jax.experimental import pallas as pl
from jax.experimental.pallas import tpu as pltpu
from jax.sharding import PartitionSpec as P

NEIGH = 72
CORES = 2
LANES = 128
WIDE = 256
UNIT = 16
WINDOW = 5
LAG = 2
EARLY = 2
LATE = 2
BLOCK = 4
STRIDE = 4
FRAMES_OF_ZERO = 5
MESH = pl.DeviceIdType.MESH


def kernel(
    chips,
    peers,
    pieces,
    feat_ref,
    slot_ref,
    near_ref,
    mask_ref,
    envelope_ref,
    frame_ref,
    mix_ref,
    zero_ref,
    one_ref,
    out_ref,
    feats,
    pair,
    own_one,
    raw_zero,
    raw_one,
    here_zero,
    here_one,
    res_zero,
    res_one,
    map_zero,
    map_one,
    local_sem,
    feat_send,
    feat_recv,
    raw_send,
    raw_recv,
    here_send,
    near_recv,
    map_send,
    map_recv,
    one_in,
    frame_ref_in,
    chosen,
    gate_ref,
    rows32,
    lined,
    turned,
    padded,
    rows_of,
    picked,
    rotated,
    paired,
    sums_zero,
    sums_one,
    full_zero,
    full_one,
    summed,
):
    experts = chips * CORES
    sys_index = lax.axis_index("sys")
    graph_index = lax.axis_index("graph")
    chip = sys_index // CORES
    core = sys_index % CORES
    last = chips - 1
    partner = chip * CORES + 1 - core
    is_inner = jnp.logical_and(chip > 0, chip < last)
    is_end = jnp.logical_or(chip == 0, chip == last)
    by_end = jnp.logical_or(chip == 1, chip == last - 1)
    end_chip = jnp.where(chip <= 1, 0, last)
    spots = peers * CORES
    my_spot = graph_index * CORES + core

    barrier = pltpu.get_barrier_semaphore()

    def greet(target_sys, target_graph):
        pl.semaphore_signal(
            barrier, inc=1, device_id=(target_sys, target_graph), device_id_type=MESH
        )

    def column(act, inner_only):
        for t in range(1 if inner_only else 0, last if inner_only else chips):
            @pl.when(chip != t)
            def _():
                for h in range(CORES):
                    act(t * CORES + h, h)

    def greet_z(target, h):
        greet(target, graph_index)

    @pl.when(is_inner)
    def _():
        column(greet_z, False)

    @pl.when(is_end)
    def _():
        column(greet_z, True)

    greet(partner, graph_index)
    for step in range(1, peers):
        for h in range(CORES):
            greet(chip * CORES + h, lax.rem(graph_index + step, peers))
    greeted = 1 + CORES * (peers - 1) + CORES * jnp.where(is_inner, chips - 1, chips - 2)

    own_zero = pltpu.make_async_copy(
        zero_ref.at[core], raw_zero.at[sys_index], local_sem.at[0]
    )
    own_feat = pltpu.make_async_copy(feat_ref, feats.at[graph_index], local_sem.at[1])
    own_frame = pltpu.make_async_copy(frame_ref, frame_ref_in, local_sem.at[2])
    own_zero.start()
    own_feat.start()
    own_frame.start()
    load_one = pltpu.make_async_copy(one_ref, one_in, local_sem.at[3])
    load_one.start()
    pl.semaphore_wait(barrier, greeted)

    def units(j):
        return pl.ds(pieces[j][1], pieces[j][2])

    def is_zero(j):
        return pieces[j][0] == "zero"

    def pick(j, zero, one):
        return zero if is_zero(j) else one

    def remote(source, target, send, recv, system, graph):
        return pltpu.make_async_remote_copy(
            src_ref=source,
            dst_ref=target,
            send_sem=send,
            recv_sem=recv,
            device_id=(system, graph),
            device_id_type=MESH,
        )

    def wait_bytes(ref, sem):
        pltpu.make_async_copy(ref, ref, sem).wait()

    def raw_copy(j, target, half):
        return remote(
            pick(j, zero_ref, own_one).at[half, units(j)],
            pick(j, raw_zero, raw_one).at[sys_index, units(j)],
            raw_send.at[j],
            raw_recv.at[j],
            target,
            graph_index,
        )

    def send_raw(j):
        column(lambda target, h: raw_copy(j, target, h).start(), True)

        @pl.when(is_inner)
        def _():
            raw_copy(j, partner, 1 - core).start()

    def wait_raw_sent(j):
        raw = pick(j, raw_zero, raw_one)
        inner = CORES * (chips - 3) + 1
        end = CORES * (chips - 2)

        @pl.when(is_inner)
        def _():
            wait_bytes(raw.at[0:inner, units(j)], raw_send.at[j])

        @pl.when(is_end)
        def _():
            wait_bytes(raw.at[0:end, units(j)], raw_send.at[j])

    def feat_copy(step):
        return remote(
            feat_ref,
            feats.at[graph_index],
            feat_send,
            feat_recv,
            sys_index,
            lax.rem(graph_index + step, peers),
        )

    zero_pieces = [j for j in range(len(pieces)) if is_zero(j)]
    one_pieces = [j for j in range(len(pieces)) if not is_zero(j)]
    for j in zero_pieces[:WINDOW]:
        send_raw(j)
    for step in range(1, peers):
        feat_copy(step).start()

    one_units, one_rows = own_one.shape[1], own_one.shape[2]
    load_one.wait()
    pair[...] = one_in[...].astype(jnp.float32)
    for half in range(CORES):
        for u in range(one_units):
            at = (half * (one_units // 2) + u // 2) * one_rows
            own_one[half, u] = pair[at : at + one_rows, u % 2, :].astype(jnp.bfloat16)
    for j in one_pieces:
        if j < WINDOW:
            send_raw(j)
    raw_one[sys_index] = own_one[core]
    own_zero.wait()

    def here_copy(j):
        return remote(
            pick(j, here_zero, here_one).at[:, units(j)],
            pick(j, res_zero, res_one).at[:, units(j)],
            here_send.at[j],
            near_recv.at[j],
            end_chip * CORES + core,
            graph_index,
        )

    def map_copy(j, h, step):
        return remote(
            pick(j, res_zero, res_one).at[h, units(j)],
            pick(j, map_zero, map_one).at[units(j), my_spot],
            map_send.at[j],
            map_recv.at[j],
            chip * CORES + h,
            lax.rem(graph_index + step, peers),
        )

    def mix_units(j, inputs, outputs):
        raw = pick(j, raw_zero, raw_one)
        _, begin, count = pieces[j][:3]
        strips = raw.shape[3] // LANES

        def body(i, carry):
            u = begin + i // strips
            lanes = pl.ds(pl.multiple_of((i % strips) * LANES, LANES), LANES)
            sums = [None] * len(outputs)
            for e in inputs:
                term = raw[e, u, :, lanes].astype(jnp.float32)
                for n, (system, _, _) in enumerate(outputs):
                    part = mix_ref[system, e] * term
                    sums[n] = part if sums[n] is None else sums[n] + part
            for n, (_, ref, at) in enumerate(outputs):
                ref[at, u, :, lanes] = sums[n].astype(jnp.bfloat16)
            return carry

        lax.fori_loop(0, count * strips, body, 0)

    def mix_all(j):
        res, here = pick(j, res_zero, res_one), pick(j, here_zero, here_one)
        mix_units(
            j,
            range(experts),
            [(chip * CORES + h, res, h) for h in range(CORES)]
            + [(end_chip * CORES + h, here, h) for h in range(CORES)],
        )

        @pl.when(by_end)
        def _():
            here_copy(j).start()

    def first_half(j):
        raw = pick(j, raw_zero, raw_one)

        @pl.when(is_inner)
        def _():
            wait_bytes(raw.at[0 : experts - 1, units(j)], raw_recv.at[j])
            mix_all(j)

    def second_half(j):
        res = pick(j, res_zero, res_one)

        @pl.when(is_end)
        def _():
            here_copy(j).wait_recv()

        for step in range(1, peers):
            for h in range(CORES):
                map_copy(j, h, step).start()
        for h in range(CORES):

            @pl.when(core != h)
            def _():
                map_copy(j, h, 0).start()

            @pl.when(core == h)
            def _():
                pick(j, map_zero, map_one)[units(j), my_spot] = res[h, units(j)]

    def wait_map(j):
        maps = pick(j, map_zero, map_one)
        wait_bytes(maps.at[units(j), 0 : spots - 1], map_recv.at[j])

    def wait_sent(j):
        if j + WINDOW >= total:
            wait_raw_sent(j)

        @pl.when(by_end)
        def _():
            here_copy(j).wait_send()

        maps = pick(j, map_zero, map_one)
        wait_bytes(maps.at[units(j), 0 : spots - 1], map_send.at[j])

    total = len(pieces)

    def advance(i):
        if i < total:
            first_half(i)
            if i + WINDOW < total:
                wait_raw_sent(i)
                send_raw(i + WINDOW)
        if LAG <= i < total + LAG:
            second_half(i - LAG)

    atoms = slot_ref.shape[1]
    edges = near_ref.shape[1]
    harmonics, frames = frame_ref.shape[0], frame_ref.shape[1]
    channels = feat_ref.shape[2]
    tiles = edges // LANES
    groups = LANES // UNIT
    spread = LANES // UNIT
    layers = -(-harmonics // spread)
    order_zero = FRAMES_OF_ZERO * channels
    side = one_ref.shape[2]
    wide = spread * LANES

    gate_ref[...] = envelope_ref[...] * mask_ref[...].astype(jnp.float32)
    by_id = (
        lax.broadcasted_iota(jnp.int32, (atoms, edges), 0) == near_ref[...]
    ).astype(jnp.bfloat16)
    by_slot = (
        lax.broadcasted_iota(jnp.int32, (atoms, atoms), 0) == slot_ref[...]
    ).astype(jnp.bfloat16)
    chosen[...] = jnp.dot(by_slot, by_id, preferred_element_type=jnp.float32).astype(
        jnp.bfloat16
    )
    own_frame.wait()

    def lay_tile(t, carry):
        lanes = pl.ds(pl.multiple_of(t * LANES, LANES), LANES)
        for m in range(layers):
            rows = pl.ds(pl.multiple_of((t * layers + m) * UNIT, UNIT), UNIT)
            for i in range(spread):
                k = m * spread + i
                at = slice(i * LANES, (i + 1) * LANES)
                if k < harmonics:
                    rows32[k, :frames] = frame_ref_in[k, :, lanes].astype(jnp.float32)
                    lined[rows, at] = rows32[k].astype(jnp.bfloat16)
                else:
                    lined[rows, at] = jnp.zeros((UNIT, LANES), jnp.bfloat16)
        for r in range(frames):
            padded[r, :harmonics, lanes] = (rows32[:, r, :] * gate_ref[:, lanes]).astype(
                jnp.bfloat16
            )
        return carry

    rows32[...] = jnp.zeros_like(rows32)
    padded[...] = jnp.zeros_like(padded)
    lax.fori_loop(0, tiles, lay_tile, 0)
    deep = padded.shape[1]
    pairs, couple = paired.shape[0], paired.shape[3]
    for p in range(pairs):
        for r in range(frames):
            paired[p, r] = padded[r, :, p * couple : (p + 1) * couple]

    def turn(n, carry):
        begin = pl.multiple_of(n * WIDE, WIDE)
        source = lax.broadcasted_iota(jnp.int32, (wide, WIDE), 0)
        target = lax.broadcasted_iota(jnp.int32, (wide, WIDE), 1) + begin
        moved = (
            source % LANES // UNIT * LANES + source // LANES * UNIT + source % UNIT
        )
        swap = (moved == target).astype(jnp.bfloat16)
        turned[:, :, pl.ds(begin, WIDE)] = jnp.dot(
            lined[...], swap, preferred_element_type=jnp.float32
        ).reshape(tiles * layers, UNIT, WIDE)
        return carry

    lax.fori_loop(0, wide // WIDE, turn, 0)
    for q in range(groups):
        picked[q, harmonics * UNIT :] = jnp.zeros(
            (picked.shape[1] - harmonics * UNIT, channels), jnp.bfloat16
        )

    for i in range(EARLY):
        advance(i)
    own_feat.wait()
    wait_bytes(feats.at[0 : peers - 1], feat_recv)
    for k in range(harmonics):
        rows_of[:, k * channels : (k + 1) * channels] = feats[:, k].reshape(atoms, channels)

    diagonal = (
        lax.broadcasted_iota(jnp.int32, (UNIT, LANES), 1) % UNIT
        == lax.broadcasted_iota(jnp.int32, (UNIT, LANES), 0)
    ).astype(jnp.float32)

    def rotate_tile(t, carry):
        lanes = pl.ds(pl.multiple_of(t * LANES, LANES), LANES)
        hot = chosen[:, lanes]
        for k in range(0, harmonics, 2):
            width = min(2, harmonics - k) * channels
            block = lax.dot_general(
                hot,
                rows_of[:, k * channels : k * channels + width],
                (((0,), (0,)), ((), ())),
                preferred_element_type=jnp.float32,
            ).astype(jnp.bfloat16)
            for q in range(groups):
                for d in range(width // channels):
                    picked[q, (k + d) * UNIT : (k + d + 1) * UNIT, :] = block[
                        q * UNIT : (q + 1) * UNIT, d * channels : (d + 1) * channels
                    ]
        for q in range(groups):
            left = []
            for r in range(frames):
                pieces_of = []
                for m in range(layers):
                    row = turned[t * layers + m, r : r + 1, q * LANES : (q + 1) * LANES]
                    pieces_of.append((row * diagonal).astype(jnp.bfloat16))
                left.append(jnp.concatenate(pieces_of, axis=1))
            result = jnp.dot(
                jnp.concatenate(left, axis=0), picked[q], preferred_element_type=jnp.float32
            ).astype(jnp.bfloat16)
            rows = pl.ds(pl.multiple_of(t * LANES + q * UNIT, UNIT), UNIT)
            for r in range(frames):
                rotated[rows, r * channels : (r + 1) * channels] = result[
                    r * UNIT : (r + 1) * UNIT
                ]
        for i in range(EARLY, total + LAG):
            if i - EARLY < tiles:

                @pl.when(t == i - EARLY)
                def _():
                    advance(i)

        return carry

    lax.fori_loop(0, tiles, rotate_tile, 0)

    second = lax.broadcasted_iota(jnp.int32, (deep, couple), 1) >= NEIGH
    quarter = (frames - FRAMES_OF_ZERO) // 2

    def masked(p, begin, end):
        left = []
        for r in range(begin, end):
            block = paired[p, r]
            nought = jnp.zeros_like(block)
            left.append(jnp.where(second, nought, block))
            left.append(jnp.where(second, block, nought))
        return jnp.concatenate(left, axis=0)

    def product(left, right):
        return jnp.dot(left, right, preferred_element_type=jnp.float32)

    def collect(p, carry):
        rows = pl.ds(pl.multiple_of(p * couple, UNIT), couple)
        result = product(
            masked(p, 0, FRAMES_OF_ZERO), rotated[rows, :order_zero]
        ).astype(jnp.bfloat16)
        for r in range(FRAMES_OF_ZERO):
            sums_zero[r, p] = result[r * 2 * deep : (r + 1) * 2 * deep]
        plus = masked(p, FRAMES_OF_ZERO, FRAMES_OF_ZERO + quarter)
        minus = masked(p, FRAMES_OF_ZERO + quarter, frames)
        x_plus = rotated[rows, order_zero : order_zero + side]
        x_minus = rotated[rows, order_zero + side : order_zero + 2 * side]
        with_real = (product(plus, x_plus) + product(minus, x_minus)).astype(jnp.bfloat16)
        with_imag = (product(minus, x_plus) - product(plus, x_minus)).astype(jnp.bfloat16)
        for r in range(quarter):
            at = slice(r * 2 * deep, (r + 1) * 2 * deep)
            sums_one[0, r, p] = with_real[at]
            sums_one[1, r, p] = with_imag[at]
        for n, i in enumerate(range(EARLY + tiles, total + LAG - LATE)):

            @pl.when(p == min(STRIDE * n + STRIDE - 2, pairs - 1))
            def _():
                advance(i)

        return carry

    lax.fori_loop(0, pairs, collect, 0)

    zero_rows = map_zero.shape[2]
    part_rows = map_one.shape[2]
    zero_count, one_count = map_zero.shape[0], map_one.shape[0]
    rows_all = pairs * 2 * deep
    nt = (((1,), (1,)), ((), ()))

    def lay_rows(store, first, block):
        done, height = 0, block.shape[0]
        while done < height:
            r, c = divmod(first + done, channels)
            count = min(height - done, channels - c)
            store(r, slice(c, c + count), block[done : done + count])
            done += count

    def lay_zero(u):
        def store(r, at, block):
            full_zero[r, at, :] = block

        for p in range(spots):
            lay_rows(store, (p * zero_count + u) * zero_rows, map_zero[u, p])

    def lay_one(u):
        def store(r, at, block):
            full_one[u % 2, r, at, :] = block

        for p in range(spots):
            lay_rows(store, (p * (one_count // 2) + u // 2) * part_rows, map_one[u, p])

    def add_frames(sums, full):
        width = sums.shape[3]

        def body(b, carry):
            total = None
            for r in range(sums.shape[0]):
                part = lax.dot_general(
                    sums[r, pl.ds(b * BLOCK, BLOCK)].reshape(BLOCK * 2 * deep, width),
                    full[r],
                    nt,
                    preferred_element_type=jnp.float32,
                )
                total = part if total is None else total + part
            rows = pl.ds(pl.multiple_of(b * BLOCK * 2 * deep, BLOCK * 2 * deep), BLOCK * 2 * deep)
            summed[rows] += total
            return carry

        lax.fori_loop(0, pairs // BLOCK, body, 0)

    summed[...] = jnp.zeros_like(summed)
    for j in zero_pieces:
        wait_map(j)
        lay_zero(pieces[j][1])
    add_frames(sums_zero, full_zero)
    first = max(EARLY + tiles, total + LAG - LATE)
    for i in range(first, total + LAG):
        advance(i)
        for j in one_pieces[2 * (i - first) : 2 * (i - first) + 2]:
            wait_map(j)
            lay_one(pieces[j][1])
    for j in one_pieces[2 * (total + LAG - first) : len(one_pieces) // 2]:
        wait_map(j)
        lay_one(pieces[j][1])
    add_frames(sums_one.at[0], full_one.at[0])
    for j in range(total - EARLY - LATE):
        wait_sent(j)
    wait_bytes(feats.at[0 : peers - 1], feat_send)
    for j in one_pieces[len(one_pieces) // 2 :]:
        wait_map(j)
        lay_one(pieces[j][1])
    add_frames(sums_one.at[1], full_one.at[1])
    scale = 1.0 / math.sqrt(NEIGH)
    summed_by_atom = summed.reshape(2 * pairs, deep, channels)
    for k in range(harmonics):
        out_ref[k] = (summed_by_atom[:, k, :] * scale).astype(jnp.bfloat16)

    for j in range(total - EARLY - LATE, total):
        wait_sent(j)


def shards(systems, peers, node_features, atom_slot, neighbour, pad_mask, envelope, wigner_rows, mix_table, zero_weight, one_weight):
    chips = systems // CORES
    frames, harmonics, edges = wigner_rows.shape[1:]
    own_atoms, _, channels = node_features.shape[1:]
    zero_rows, zero_width = zero_weight.shape[1:]
    one_rows, _, side = one_weight.shape[1:]
    zero_units = max(1, zero_rows // (CORES * UNIT)) if zero_rows % (CORES * UNIT) == 0 else 1
    one_units = 2 * (max(1, one_rows // (CORES * UNIT)) if one_rows % (CORES * UNIT) == 0 else 1)
    zr = zero_rows // (CORES * zero_units)
    orr = 2 * one_rows // (CORES * one_units)
    pieces = tuple(("zero", u, 1) for u in range(zero_units)) + tuple(
        ("one", u, 1) for part in range(2) for u in range(part, one_units, 2)
    )
    atoms = own_atoms * peers
    layers = -(-harmonics // (LANES // UNIT))
    tiles = edges // LANES
    deep = -(-harmonics // 16) * 16
    spots = peers * CORES
    bf16, f32 = jnp.bfloat16, jnp.float32
    vmem = pl.BlockSpec(memory_space=pltpu.VMEM)
    hbm = pl.BlockSpec(memory_space=pl.ANY)
    smem = pl.BlockSpec(memory_space=pltpu.SMEM)
    count = len(pieces)
    update = pl.pallas_call(
        functools.partial(kernel, chips, peers, pieces),
        out_shape=jax.ShapeDtypeStruct((harmonics, own_atoms, channels), bf16),
        in_specs=[hbm, vmem, vmem, vmem, vmem, hbm, smem, hbm, hbm],
        out_specs=vmem,
        scratch_shapes=[
            pltpu.VMEM((peers, harmonics, own_atoms, channels), bf16),
            pltpu.VMEM((one_rows, 2, side), f32),
            pltpu.VMEM((CORES, one_units, orr, side), bf16),
            pltpu.VMEM((systems, zero_units, zr, zero_width), bf16),
            pltpu.VMEM((systems, one_units, orr, side), bf16),
            pltpu.VMEM((CORES, zero_units, zr, zero_width), bf16),
            pltpu.VMEM((CORES, one_units, orr, side), bf16),
            pltpu.VMEM((CORES, zero_units, zr, zero_width), bf16),
            pltpu.VMEM((CORES, one_units, orr, side), bf16),
            pltpu.VMEM((zero_units, spots, zr, zero_width), bf16),
            pltpu.VMEM((one_units, spots, orr, side), bf16),
            pltpu.SemaphoreType.DMA((4,)),
            pltpu.SemaphoreType.DMA,
            pltpu.SemaphoreType.DMA,
            pltpu.SemaphoreType.DMA((count,)),
            pltpu.SemaphoreType.DMA((count,)),
            pltpu.SemaphoreType.DMA((count,)),
            pltpu.SemaphoreType.DMA((count,)),
            pltpu.SemaphoreType.DMA((count,)),
            pltpu.SemaphoreType.DMA((count,)),
            pltpu.VMEM((one_rows, 2, side), bf16),
            pltpu.VMEM((harmonics, frames, edges), bf16),
            pltpu.VMEM((atoms, edges), bf16),
            pltpu.VMEM((1, edges), f32),
            pltpu.VMEM((harmonics, UNIT, LANES), f32),
            pltpu.VMEM((tiles * layers * UNIT, LANES // UNIT * LANES), bf16),
            pltpu.VMEM((tiles * layers, UNIT, LANES // UNIT * LANES), f32),
            pltpu.VMEM((frames, deep, edges), bf16),
            pltpu.VMEM((atoms, harmonics * channels), bf16),
            pltpu.VMEM((LANES // UNIT, layers * LANES, channels), bf16),
            pltpu.VMEM((edges, frames * channels), bf16),
            pltpu.VMEM((own_atoms // 2, frames, deep, 2 * NEIGH), bf16),
            pltpu.VMEM((FRAMES_OF_ZERO, own_atoms // 2, 2 * deep, zero_width), bf16),
            pltpu.VMEM((2, (frames - FRAMES_OF_ZERO) // 2, own_atoms // 2, 2 * deep, side), bf16),
            pltpu.VMEM((FRAMES_OF_ZERO, channels, zero_width), bf16),
            pltpu.VMEM((2, (frames - FRAMES_OF_ZERO) // 2, channels, side), bf16),
            pltpu.VMEM((own_atoms * deep, channels), f32),
        ],
        compiler_params=pltpu.CompilerParams(
            collective_id=0, has_side_effects=True, vmem_limit_bytes=60 * 1024 * 1024
        ),
        name="edge_convolution",
    )(
        jnp.transpose(node_features[0], (1, 0, 2)),
        atom_slot,
        neighbour,
        pad_mask,
        envelope,
        jnp.transpose(wigner_rows[0], (1, 0, 2)),
        mix_table,
        zero_weight[0].reshape(CORES, zero_units, zr, zero_width),
        one_weight[0],
    )
    return jnp.transpose(update, (1, 0, 2))[None]


def solution(mesh):
    return jax.shard_map(
        functools.partial(shards, mesh.shape["sys"], mesh.shape["graph"]),
        mesh=mesh,
        in_specs=(
            P("sys", "graph", None, None),
            P("sys", None),
            P("sys", "graph"),
            P("sys", "graph"),
            P("sys", "graph"),
            P("sys", None, None, "graph"),
            P(),
            P("sys", "graph", None),
            P("sys", "graph", None, None),
        ),
        out_specs=P("sys", "graph", None, None),
        check_vma=False,
    )
```

```python
import functools
import math

import jax
import jax.numpy as jnp
from jax import lax
from jax.experimental import pallas as pl
from jax.experimental.pallas import tpu as pltpu
from jax.sharding import PartitionSpec as P

NEIGH = 72
CORES = 2
LANES = 128
WIDE = 256
UNIT = 16
WINDOW = 5
LAG = 3
EARLY = 2
LATE = 2
BLOCK = 4
STRIDE = 3
FRAMES_OF_ZERO = 5
MESH = pl.DeviceIdType.MESH


def kernel(
    chips,
    peers,
    pieces,
    feat_ref,
    slot_ref,
    near_ref,
    mask_ref,
    envelope_ref,
    frame_ref,
    mix_ref,
    zero_ref,
    one_ref,
    out_ref,
    feats,
    pair,
    own_one,
    raw_zero,
    raw_one,
    here_zero,
    here_one,
    res_zero,
    res_one,
    map_zero,
    map_one,
    local_sem,
    feat_send,
    feat_recv,
    raw_send,
    raw_recv,
    here_send,
    near_recv,
    map_send,
    map_recv,
    one_in,
    frame_ref_in,
    chosen,
    gate_ref,
    rows32,
    lined,
    turned,
    padded,
    rows_of,
    picked,
    rotated,
    paired,
    sums_zero,
    sums_one,
    full_zero,
    full_one,
    summed,
):
    experts = chips * CORES
    sys_index = lax.axis_index("sys")
    graph_index = lax.axis_index("graph")
    chip = sys_index // CORES
    core = sys_index % CORES
    last = chips - 1
    partner = chip * CORES + 1 - core
    is_inner = jnp.logical_and(chip > 0, chip < last)
    is_end = jnp.logical_or(chip == 0, chip == last)
    by_end = jnp.logical_or(chip == 1, chip == last - 1)
    end_chip = jnp.where(chip <= 1, 0, last)
    spots = peers * CORES
    my_spot = graph_index * CORES + core

    barrier = pltpu.get_barrier_semaphore()

    def greet(target_sys, target_graph):
        pl.semaphore_signal(
            barrier, inc=1, device_id=(target_sys, target_graph), device_id_type=MESH
        )

    def column(act, inner_only):
        for t in range(1 if inner_only else 0, last if inner_only else chips):
            @pl.when(chip != t)
            def _():
                for h in range(CORES):
                    act(t * CORES + h, h)

    def greet_z(target, h):
        greet(target, graph_index)

    @pl.when(is_inner)
    def _():
        column(greet_z, False)

    @pl.when(is_end)
    def _():
        column(greet_z, True)

    greet(partner, graph_index)
    for step in range(1, peers):
        for h in range(CORES):
            greet(chip * CORES + h, lax.rem(graph_index + step, peers))
    greeted = 1 + CORES * (peers - 1) + CORES * jnp.where(is_inner, chips - 1, chips - 2)

    own_zero = pltpu.make_async_copy(
        zero_ref.at[core], raw_zero.at[sys_index], local_sem.at[0]
    )
    own_feat = pltpu.make_async_copy(feat_ref, feats.at[graph_index], local_sem.at[1])
    own_frame = pltpu.make_async_copy(frame_ref, frame_ref_in, local_sem.at[2])
    own_zero.start()
    own_feat.start()
    own_frame.start()
    load_one = pltpu.make_async_copy(one_ref, one_in, local_sem.at[3])
    load_one.start()
    pl.semaphore_wait(barrier, greeted)

    def units(j):
        return pl.ds(pieces[j][1], pieces[j][2])

    def is_zero(j):
        return pieces[j][0] == "zero"

    def pick(j, zero, one):
        return zero if is_zero(j) else one

    def remote(source, target, send, recv, system, graph):
        return pltpu.make_async_remote_copy(
            src_ref=source,
            dst_ref=target,
            send_sem=send,
            recv_sem=recv,
            device_id=(system, graph),
            device_id_type=MESH,
        )

    def wait_bytes(ref, sem):
        pltpu.make_async_copy(ref, ref, sem).wait()

    def raw_copy(j, target, half):
        return remote(
            pick(j, zero_ref, own_one).at[half, units(j)],
            pick(j, raw_zero, raw_one).at[sys_index, units(j)],
            raw_send.at[j],
            raw_recv.at[j],
            target,
            graph_index,
        )

    def send_raw(j):
        column(lambda target, h: raw_copy(j, target, h).start(), True)

        @pl.when(is_inner)
        def _():
            raw_copy(j, partner, 1 - core).start()

    def wait_raw_sent(j):
        raw = pick(j, raw_zero, raw_one)
        inner = CORES * (chips - 3) + 1
        end = CORES * (chips - 2)

        @pl.when(is_inner)
        def _():
            wait_bytes(raw.at[0:inner, units(j)], raw_send.at[j])

        @pl.when(is_end)
        def _():
            wait_bytes(raw.at[0:end, units(j)], raw_send.at[j])

    def feat_copy(step):
        return remote(
            feat_ref,
            feats.at[graph_index],
            feat_send,
            feat_recv,
            sys_index,
            lax.rem(graph_index + step, peers),
        )

    zero_pieces = [j for j in range(len(pieces)) if is_zero(j)]
    one_pieces = [j for j in range(len(pieces)) if not is_zero(j)]
    for j in zero_pieces[:WINDOW]:
        send_raw(j)
    for step in range(1, peers):
        feat_copy(step).start()

    one_units, one_rows = own_one.shape[1], own_one.shape[2]
    load_one.wait()
    pair[...] = one_in[...].astype(jnp.float32)
    for half in range(CORES):
        for u in range(one_units):
            at = (half * (one_units // 2) + u // 2) * one_rows
            own_one[half, u] = pair[at : at + one_rows, u % 2, :].astype(jnp.bfloat16)
    for j in one_pieces:
        if j < WINDOW:
            send_raw(j)
    raw_one[sys_index] = own_one[core]
    own_zero.wait()

    def here_copy(j):
        return remote(
            pick(j, here_zero, here_one).at[:, units(j)],
            pick(j, res_zero, res_one).at[:, units(j)],
            here_send.at[j],
            near_recv.at[j],
            end_chip * CORES + core,
            graph_index,
        )

    def map_copy(j, h, step):
        return remote(
            pick(j, res_zero, res_one).at[h, units(j)],
            pick(j, map_zero, map_one).at[units(j), my_spot],
            map_send.at[j],
            map_recv.at[j],
            chip * CORES + h,
            lax.rem(graph_index + step, peers),
        )

    def mix_units(j, inputs, outputs):
        raw = pick(j, raw_zero, raw_one)
        _, begin, count = pieces[j][:3]
        strips = raw.shape[3] // LANES

        def body(i, carry):
            u = begin + i // strips
            lanes = pl.ds(pl.multiple_of((i % strips) * LANES, LANES), LANES)
            sums = [None] * len(outputs)
            for e in inputs:
                term = raw[e, u, :, lanes].astype(jnp.float32)
                for n, (system, _, _) in enumerate(outputs):
                    part = mix_ref[system, e] * term
                    sums[n] = part if sums[n] is None else sums[n] + part
            for n, (_, ref, at) in enumerate(outputs):
                ref[at, u, :, lanes] = sums[n].astype(jnp.bfloat16)
            return carry

        lax.fori_loop(0, count * strips, body, 0)

    def mix_all(j):
        res, here = pick(j, res_zero, res_one), pick(j, here_zero, here_one)
        mix_units(
            j,
            range(experts),
            [(chip * CORES + h, res, h) for h in range(CORES)]
            + [(end_chip * CORES + h, here, h) for h in range(CORES)],
        )

        @pl.when(by_end)
        def _():
            here_copy(j).start()

    def first_half(j):
        raw = pick(j, raw_zero, raw_one)

        @pl.when(is_inner)
        def _():
            wait_bytes(raw.at[0 : experts - 1, units(j)], raw_recv.at[j])
            mix_all(j)

    def second_half(j):
        res = pick(j, res_zero, res_one)

        @pl.when(is_end)
        def _():
            here_copy(j).wait_recv()

        for step in range(1, peers):
            for h in range(CORES):
                map_copy(j, h, step).start()
        for h in range(CORES):

            @pl.when(core != h)
            def _():
                map_copy(j, h, 0).start()

            @pl.when(core == h)
            def _():
                pick(j, map_zero, map_one)[units(j), my_spot] = res[h, units(j)]

    def wait_map(j):
        maps = pick(j, map_zero, map_one)
        wait_bytes(maps.at[units(j), 0 : spots - 1], map_recv.at[j])

    def wait_sent(j):
        if j + WINDOW >= total:
            wait_raw_sent(j)

        @pl.when(by_end)
        def _():
            here_copy(j).wait_send()

        maps = pick(j, map_zero, map_one)
        wait_bytes(maps.at[units(j), 0 : spots - 1], map_send.at[j])

    total = len(pieces)

    def advance(i):
        if i < total:
            first_half(i)
            if i + WINDOW < total:
                wait_raw_sent(i)
                send_raw(i + WINDOW)
        if LAG <= i < total + LAG:
            second_half(i - LAG)

    atoms = slot_ref.shape[1]
    edges = near_ref.shape[1]
    harmonics, frames = frame_ref.shape[0], frame_ref.shape[1]
    channels = feat_ref.shape[2]
    tiles = edges // LANES
    groups = LANES // UNIT
    spread = LANES // UNIT
    layers = -(-harmonics // spread)
    order_zero = FRAMES_OF_ZERO * channels
    side = one_ref.shape[2]
    wide = spread * LANES

    gate_ref[...] = envelope_ref[...] * mask_ref[...].astype(jnp.float32)
    by_id = (
        lax.broadcasted_iota(jnp.int32, (atoms, edges), 0) == near_ref[...]
    ).astype(jnp.bfloat16)
    by_slot = (
        lax.broadcasted_iota(jnp.int32, (atoms, atoms), 0) == slot_ref[...]
    ).astype(jnp.bfloat16)
    chosen[...] = jnp.dot(by_slot, by_id, preferred_element_type=jnp.float32).astype(
        jnp.bfloat16
    )
    own_frame.wait()

    def lay_tile(t, carry):
        lanes = pl.ds(pl.multiple_of(t * LANES, LANES), LANES)
        for m in range(layers):
            rows = pl.ds(pl.multiple_of((t * layers + m) * UNIT, UNIT), UNIT)
            for i in range(spread):
                k = m * spread + i
                at = slice(i * LANES, (i + 1) * LANES)
                if k < harmonics:
                    rows32[k, :frames] = frame_ref_in[k, :, lanes].astype(jnp.float32)
                    lined[rows, at] = rows32[k].astype(jnp.bfloat16)
                else:
                    lined[rows, at] = jnp.zeros((UNIT, LANES), jnp.bfloat16)
        for r in range(frames):
            padded[r, :harmonics, lanes] = (rows32[:, r, :] * gate_ref[:, lanes]).astype(
                jnp.bfloat16
            )
        return carry

    rows32[...] = jnp.zeros_like(rows32)
    padded[...] = jnp.zeros_like(padded)
    lax.fori_loop(0, tiles, lay_tile, 0)
    deep = padded.shape[1]
    pairs, couple = paired.shape[0], paired.shape[3]
    for p in range(pairs):
        for r in range(frames):
            paired[p, r] = padded[r, :, p * couple : (p + 1) * couple]

    def turn(n, carry):
        begin = pl.multiple_of(n * WIDE, WIDE)
        source = lax.broadcasted_iota(jnp.int32, (wide, WIDE), 0)
        target = lax.broadcasted_iota(jnp.int32, (wide, WIDE), 1) + begin
        moved = (
            source % LANES // UNIT * LANES + source // LANES * UNIT + source % UNIT
        )
        swap = (moved == target).astype(jnp.bfloat16)
        turned[:, :, pl.ds(begin, WIDE)] = jnp.dot(
            lined[...], swap, preferred_element_type=jnp.float32
        ).reshape(tiles * layers, UNIT, WIDE)
        return carry

    advance(0)
    lax.fori_loop(0, wide // WIDE, turn, 0)
    for q in range(groups):
        picked[q, harmonics * UNIT :] = jnp.zeros(
            (picked.shape[1] - harmonics * UNIT, channels), jnp.bfloat16
        )

    for i in range(1, EARLY):
        advance(i)
    own_feat.wait()
    wait_bytes(feats.at[0 : peers - 1], feat_recv)
    for k in range(harmonics):
        rows_of[:, k * channels : (k + 1) * channels] = feats[:, k].reshape(atoms, channels)

    diagonal = (
        lax.broadcasted_iota(jnp.int32, (UNIT, LANES), 1) % UNIT
        == lax.broadcasted_iota(jnp.int32, (UNIT, LANES), 0)
    ).astype(jnp.float32)

    def rotate_tile(t, carry):
        lanes = pl.ds(pl.multiple_of(t * LANES, LANES), LANES)
        hot = chosen[:, lanes]
        for k in range(0, harmonics, 2):
            width = min(2, harmonics - k) * channels
            block = lax.dot_general(
                hot,
                rows_of[:, k * channels : k * channels + width],
                (((0,), (0,)), ((), ())),
                preferred_element_type=jnp.float32,
            ).astype(jnp.bfloat16)
            for q in range(groups):
                for d in range(width // channels):
                    picked[q, (k + d) * UNIT : (k + d + 1) * UNIT, :] = block[
                        q * UNIT : (q + 1) * UNIT, d * channels : (d + 1) * channels
                    ]
        for q in range(groups):
            left = []
            for r in range(frames):
                pieces_of = []
                for m in range(layers):
                    row = turned[t * layers + m, r : r + 1, q * LANES : (q + 1) * LANES]
                    pieces_of.append((row * diagonal).astype(jnp.bfloat16))
                left.append(jnp.concatenate(pieces_of, axis=1))
            result = jnp.dot(
                jnp.concatenate(left, axis=0), picked[q], preferred_element_type=jnp.float32
            ).astype(jnp.bfloat16)
            rows = pl.ds(pl.multiple_of(t * LANES + q * UNIT, UNIT), UNIT)
            for r in range(frames):
                rotated[rows, r * channels : (r + 1) * channels] = result[
                    r * UNIT : (r + 1) * UNIT
                ]
        for i in range(EARLY, total + LAG):
            if i - EARLY < tiles:

                @pl.when(t == i - EARLY)
                def _():
                    advance(i)

        return carry

    lax.fori_loop(0, tiles, rotate_tile, 0)

    second = lax.broadcasted_iota(jnp.int32, (deep, couple), 1) >= NEIGH
    quarter = (frames - FRAMES_OF_ZERO) // 2

    def masked(p, begin, end):
        left = []
        for r in range(begin, end):
            block = paired[p, r]
            nought = jnp.zeros_like(block)
            left.append(jnp.where(second, nought, block))
            left.append(jnp.where(second, block, nought))
        return jnp.concatenate(left, axis=0)

    def product(left, right):
        return jnp.dot(left, right, preferred_element_type=jnp.float32)

    def collect(p, carry):
        rows = pl.ds(pl.multiple_of(p * couple, UNIT), couple)
        result = product(
            masked(p, 0, FRAMES_OF_ZERO), rotated[rows, :order_zero]
        ).astype(jnp.bfloat16)
        for r in range(FRAMES_OF_ZERO):
            sums_zero[r, p] = result[r * 2 * deep : (r + 1) * 2 * deep]
        plus = masked(p, FRAMES_OF_ZERO, FRAMES_OF_ZERO + quarter)
        minus = masked(p, FRAMES_OF_ZERO + quarter, frames)
        x_plus = rotated[rows, order_zero : order_zero + side]
        x_minus = rotated[rows, order_zero + side : order_zero + 2 * side]
        with_real = (product(plus, x_plus) + product(minus, x_minus)).astype(jnp.bfloat16)
        with_imag = (product(minus, x_plus) - product(plus, x_minus)).astype(jnp.bfloat16)
        for r in range(quarter):
            at = slice(r * 2 * deep, (r + 1) * 2 * deep)
            sums_one[0, r, p] = with_real[at]
            sums_one[1, r, p] = with_imag[at]
        for n, i in enumerate(range(EARLY + tiles, total + LAG - LATE)):

            @pl.when(p == min(STRIDE * n + STRIDE - 2, pairs - 1))
            def _():
                advance(i)

        return carry

    lax.fori_loop(0, pairs, collect, 0)

    zero_rows = map_zero.shape[2]
    part_rows = map_one.shape[2]
    zero_count, one_count = map_zero.shape[0], map_one.shape[0]
    rows_all = pairs * 2 * deep
    nt = (((1,), (1,)), ((), ()))

    def lay_rows(store, first, block):
        done, height = 0, block.shape[0]
        while done < height:
            r, c = divmod(first + done, channels)
            count = min(height - done, channels - c)
            store(r, slice(c, c + count), block[done : done + count])
            done += count

    def lay_zero(u):
        def store(r, at, block):
            full_zero[r, at, :] = block

        for p in range(spots):
            lay_rows(store, (p * zero_count + u) * zero_rows, map_zero[u, p])

    def lay_one(u):
        def store(r, at, block):
            full_one[u % 2, r, at, :] = block

        for p in range(spots):
            lay_rows(store, (p * (one_count // 2) + u // 2) * part_rows, map_one[u, p])

    def add_frames(sums, full):
        width = sums.shape[3]

        def body(b, carry):
            total = None
            for r in range(sums.shape[0]):
                part = lax.dot_general(
                    sums[r, pl.ds(b * BLOCK, BLOCK)].reshape(BLOCK * 2 * deep, width),
                    full[r],
                    nt,
                    preferred_element_type=jnp.float32,
                )
                total = part if total is None else total + part
            rows = pl.ds(pl.multiple_of(b * BLOCK * 2 * deep, BLOCK * 2 * deep), BLOCK * 2 * deep)
            summed[rows] += total
            return carry

        lax.fori_loop(0, pairs // BLOCK, body, 0)

    summed[...] = jnp.zeros_like(summed)
    for j in zero_pieces:
        wait_map(j)
        lay_zero(pieces[j][1])
    add_frames(sums_zero, full_zero)
    first = max(EARLY + tiles, total + LAG - LATE)
    for i in range(first, total + LAG):
        advance(i)
        for j in one_pieces[2 * (i - first) : 2 * (i - first) + 2]:
            wait_map(j)
            lay_one(pieces[j][1])
    for j in one_pieces[2 * (total + LAG - first) : len(one_pieces) // 2]:
        wait_map(j)
        lay_one(pieces[j][1])
    add_frames(sums_one.at[0], full_one.at[0])
    for j in range(total - EARLY - LATE):
        wait_sent(j)
    wait_bytes(feats.at[0 : peers - 1], feat_send)
    for j in one_pieces[len(one_pieces) // 2 :]:
        wait_map(j)
        lay_one(pieces[j][1])
    add_frames(sums_one.at[1], full_one.at[1])
    scale = 1.0 / math.sqrt(NEIGH)
    summed_by_atom = summed.reshape(2 * pairs, deep, channels)
    for k in range(harmonics):
        out_ref[k] = (summed_by_atom[:, k, :] * scale).astype(jnp.bfloat16)

    for j in range(total - EARLY - LATE, total):
        wait_sent(j)


def shards(systems, peers, node_features, atom_slot, neighbour, pad_mask, envelope, wigner_rows, mix_table, zero_weight, one_weight):
    chips = systems // CORES
    frames, harmonics, edges = wigner_rows.shape[1:]
    own_atoms, _, channels = node_features.shape[1:]
    zero_rows, zero_width = zero_weight.shape[1:]
    one_rows, _, side = one_weight.shape[1:]
    zero_units = max(1, zero_rows // (CORES * UNIT)) if zero_rows % (CORES * UNIT) == 0 else 1
    one_units = 2 * (max(1, one_rows // (CORES * UNIT)) if one_rows % (CORES * UNIT) == 0 else 1)
    zr = zero_rows // (CORES * zero_units)
    orr = 2 * one_rows // (CORES * one_units)
    pieces = tuple(("zero", u, 1) for u in range(zero_units)) + tuple(
        ("one", u, 1) for part in range(2) for u in range(part, one_units, 2)
    )
    atoms = own_atoms * peers
    layers = -(-harmonics // (LANES // UNIT))
    tiles = edges // LANES
    deep = -(-harmonics // 16) * 16
    spots = peers * CORES
    bf16, f32 = jnp.bfloat16, jnp.float32
    vmem = pl.BlockSpec(memory_space=pltpu.VMEM)
    hbm = pl.BlockSpec(memory_space=pl.ANY)
    smem = pl.BlockSpec(memory_space=pltpu.SMEM)
    count = len(pieces)
    update = pl.pallas_call(
        functools.partial(kernel, chips, peers, pieces),
        out_shape=jax.ShapeDtypeStruct((harmonics, own_atoms, channels), bf16),
        in_specs=[hbm, vmem, vmem, vmem, vmem, hbm, smem, hbm, hbm],
        out_specs=vmem,
        scratch_shapes=[
            pltpu.VMEM((peers, harmonics, own_atoms, channels), bf16),
            pltpu.VMEM((one_rows, 2, side), f32),
            pltpu.VMEM((CORES, one_units, orr, side), bf16),
            pltpu.VMEM((systems, zero_units, zr, zero_width), bf16),
            pltpu.VMEM((systems, one_units, orr, side), bf16),
            pltpu.VMEM((CORES, zero_units, zr, zero_width), bf16),
            pltpu.VMEM((CORES, one_units, orr, side), bf16),
            pltpu.VMEM((CORES, zero_units, zr, zero_width), bf16),
            pltpu.VMEM((CORES, one_units, orr, side), bf16),
            pltpu.VMEM((zero_units, spots, zr, zero_width), bf16),
            pltpu.VMEM((one_units, spots, orr, side), bf16),
            pltpu.SemaphoreType.DMA((4,)),
            pltpu.SemaphoreType.DMA,
            pltpu.SemaphoreType.DMA,
            pltpu.SemaphoreType.DMA((count,)),
            pltpu.SemaphoreType.DMA((count,)),
            pltpu.SemaphoreType.DMA((count,)),
            pltpu.SemaphoreType.DMA((count,)),
            pltpu.SemaphoreType.DMA((count,)),
            pltpu.SemaphoreType.DMA((count,)),
            pltpu.VMEM((one_rows, 2, side), bf16),
            pltpu.VMEM((harmonics, frames, edges), bf16),
            pltpu.VMEM((atoms, edges), bf16),
            pltpu.VMEM((1, edges), f32),
            pltpu.VMEM((harmonics, UNIT, LANES), f32),
            pltpu.VMEM((tiles * layers * UNIT, LANES // UNIT * LANES), bf16),
            pltpu.VMEM((tiles * layers, UNIT, LANES // UNIT * LANES), f32),
            pltpu.VMEM((frames, deep, edges), bf16),
            pltpu.VMEM((atoms, harmonics * channels), bf16),
            pltpu.VMEM((LANES // UNIT, layers * LANES, channels), bf16),
            pltpu.VMEM((edges, frames * channels), bf16),
            pltpu.VMEM((own_atoms // 2, frames, deep, 2 * NEIGH), bf16),
            pltpu.VMEM((FRAMES_OF_ZERO, own_atoms // 2, 2 * deep, zero_width), bf16),
            pltpu.VMEM((2, (frames - FRAMES_OF_ZERO) // 2, own_atoms // 2, 2 * deep, side), bf16),
            pltpu.VMEM((FRAMES_OF_ZERO, channels, zero_width), bf16),
            pltpu.VMEM((2, (frames - FRAMES_OF_ZERO) // 2, channels, side), bf16),
            pltpu.VMEM((own_atoms * deep, channels), f32),
        ],
        compiler_params=pltpu.CompilerParams(
            collective_id=0, has_side_effects=True, vmem_limit_bytes=60 * 1024 * 1024
        ),
        name="edge_convolution",
    )(
        jnp.transpose(node_features[0], (1, 0, 2)),
        atom_slot,
        neighbour,
        pad_mask,
        envelope,
        jnp.transpose(wigner_rows[0], (1, 0, 2)),
        mix_table,
        zero_weight[0].reshape(CORES, zero_units, zr, zero_width),
        one_weight[0],
    )
    return jnp.transpose(update, (1, 0, 2))[None]


def solution(mesh):
    return jax.shard_map(
        functools.partial(shards, mesh.shape["sys"], mesh.shape["graph"]),
        mesh=mesh,
        in_specs=(
            P("sys", "graph", None, None),
            P("sys", None),
            P("sys", "graph"),
            P("sys", "graph"),
            P("sys", "graph"),
            P("sys", None, None, "graph"),
            P(),
            P("sys", "graph", None),
            P("sys", "graph", None, None),
        ),
        out_specs=P("sys", "graph", None, None),
        check_vma=False,
    )
```
